512 devices in a mesh: fsdp: 128 (over x, z, core), rep: 4 (over y).
Axes of the slice: x: 4, y: 4, z: 16, core: 2. Of those that a mesh axis runs over, the one named last changes fastest.
Arguments:
- grads: bfloat16 [128, 1024, 768], P('rep', 'fsdp'), may hold values from -6 to 6
- momentum: float32 [128, 1024, 768], P('rep', 'fsdp'), may hold values from -6 to 6
- master: float32 [128, 1024, 768], P('rep', 'fsdp'), may hold values from -0.1875 to 0.1875
- owners: int32 [128], replicated, may hold values from 0 to 127, as said below
- offsets: int32 [128], replicated, may hold values from 0 to 127
Outputs:
- new_momentum: float32 [128, 1024, 768], P('rep', 'fsdp')
- new_master: float32 [128, 1024, 768], P('rep', 'fsdp')
- weights: bfloat16 [128, 1024, 768], P(None, 'fsdp')
- slot_rms: float32 [128, 4], P('fsdp', 'rep')
The draws below stay inside these ranges and needn't reach their ends.
Inputs may be any that keep to these rules, and one draw needn't show every extreme that they name: `owners`: within each aligned block of 32 matrices, no two matrices name the same owner index.
All inputs are finite; a program needn't handle non-finite values.
Results may differ from the reference program's by a relative error of at most 0.0013.
Values may be sent and summed in bfloat16 or wider, within the bound.
A program may use at most 64 MiB of HBM per device.

```python
import math
import jax
import jax.numpy as jnp
from jax import lax

D = 1024
FF = 768
ITERS = 2
MATS_BLK = 32
MATS = 128
N_FSDP = 128
N_REP = 4


def draw_owners(key, part):
    block_keys = jax.random.split(jax.random.fold_in(key, 17), N_REP)

    def one_block(block_key):
        return jax.random.permutation(block_key, N_FSDP)[:MATS_BLK].astype(jnp.int32)
    return jax.vmap(one_block)(block_keys).reshape(MATS)


def place_ends(entries, rng, smallest, top_value):
    dims = entries.shape
    index_at = [jax.random.randint(jax.random.fold_in(rng, axis), (), 0, dims[axis]) for axis in range(len(dims))]
    entries = entries.at[tuple(index_at)].set(smallest)
    longest = dims.index(max(dims))
    index_at[longest] = (index_at[longest] + 1) % dims[longest]
    return entries.at[tuple(index_at)].set(top_value)


def steps_of(own_key, shape, cuts, smallest, top_value):
    level, own = 1.0, jax.random.fold_in(own_key, 6)
    for dim, shards_of in cuts:
        draws = jnp.exp(jax.random.uniform(jax.random.fold_in(own, dim), (shards_of,), jnp.float32, smallest / len(cuts), top_value / len(cuts)))
        level = level * jnp.repeat(draws, shape[dim] // shards_of).reshape([-1 if axis == dim else 1 for axis in range(len(shape))])
    return level


def centred(key, dims, spread, limit, shards=(), kind=jnp.bfloat16):
    loudness = steps_of(key, dims, shards, -0.22, 0.18) if shards else 1.0
    array = jax.random.normal(key, dims, jnp.float32) * spread * loudness
    return jnp.minimum(jnp.maximum(array, -limit), limit).astype(kind)


def setup_inputs(seed: int = 0) -> dict:
    key_list = jax.random.split(jax.random.key(seed), 6)
    grads = centred(key_list[0], (MATS, D, FF), 1.0, 6.0, ((0, 4), (1, 128)))
    momentum = centred(key_list[1], (MATS, D, FF), 1.0, 6.0, ((0, 4), (1, 128)), jnp.float32)
    master = centred(key_list[2], (MATS, D, FF), D ** -0.5, 0.1875, ((0, 4), (1, 128)), jnp.float32)
    owners = draw_owners(jax.random.fold_in(key_list[5], 71), 0)
    offsets = place_ends(jax.random.randint(key_list[4], (MATS,), 0, N_FSDP), jax.random.fold_in(key_list[4], 1), 0, N_FSDP - 1).astype(jnp.int32)
    return dict(grads=grads, momentum=momentum, master=master, owners=owners, offsets=offsets)


COEF_FIRST = 3.4445
COEF_SECOND = -4.775
COEF_THIRD = 2.0315
MOMENTUM_DECAY = 0.95
LEARN_RATE = 0.02
DECAY_RATE = 0.1
EPSILON = 1e-07

def polish(matrix):
    frobenius = jnp.sqrt(jnp.sum(jnp.square(matrix.astype(jnp.float32))))
    iterate = (matrix.astype(jnp.float32) / (frobenius + EPSILON)).astype(jnp.bfloat16)
    iterate = lax.optimization_barrier(iterate)
    for _ in range(ITERS):
        gram_matrix = lax.dot_general(iterate, iterate, (((0,), (0,)), ((), ())), preferred_element_type=jnp.float32).astype(jnp.bfloat16)
        gram_matrix = lax.optimization_barrier(gram_matrix)
        polynomial = (COEF_SECOND * gram_matrix.astype(jnp.float32) + COEF_THIRD * jnp.dot(gram_matrix, gram_matrix, preferred_element_type=jnp.float32)).astype(jnp.bfloat16)
        iterate = (COEF_FIRST * iterate.astype(jnp.float32) + jnp.dot(iterate, polynomial, preferred_element_type=jnp.float32)).astype(jnp.bfloat16)
        iterate = lax.optimization_barrier(iterate)
    return (iterate, frobenius)

def reference(grads, momentum, master, owners, offsets):
    row_count = D // N_FSDP
    new_momentum = MOMENTUM_DECAY * momentum + grads.astype(jnp.float32)
    half = new_momentum.astype(jnp.bfloat16)

    def polish_one(entry_pair):
        matrix, offset_value = entry_pair
        blocks = matrix.reshape(N_FSDP, row_count, FF)
        ordered = jnp.roll(blocks, offset_value, axis=0).reshape(D, FF)
        iterate, frobenius = polish(ordered)
        stored = jnp.roll(iterate.reshape(N_FSDP, row_count, FF), -offset_value, axis=0).reshape(D, FF)
        return (stored, frobenius)
    polished, norms = lax.map(polish_one, (half, offsets))
    update = 0.2 * math.sqrt(max(D, FF)) * polished.astype(jnp.float32)
    new_master = master - LEARN_RATE * (update + DECAY_RATE * master)
    weight_rows = new_master.astype(jnp.bfloat16)

    def reorder(entry_pair):
        matrix, offset_value = entry_pair
        return jnp.roll(matrix.reshape(N_FSDP, row_count, FF), offset_value, axis=0).reshape(D, FF)
    weights = lax.map(reorder, (weight_rows, offsets))
    positions = jnp.arange(MATS, dtype=jnp.int32)
    block_of = positions // MATS_BLK
    owner_table = (owners[:, None] == jnp.arange(N_FSDP, dtype=jnp.int32)[None, :]).astype(jnp.float32)
    block_table = (block_of[:, None] == jnp.arange(N_REP, dtype=jnp.int32)[None, :]).astype(jnp.float32)
    rms_values = norms / math.sqrt(D * FF)
    slot_rms = jnp.einsum('mo,ms->os', owner_table * rms_values[:, None], block_table)
    return (new_momentum, new_master, weights, slot_rms)
```

```python
import math

import jax
import jax.numpy as jnp
from jax import lax
from jax.sharding import Mesh, PartitionSpec as P

ITERS = 2

COEF_FIRST = 3.4445
COEF_SECOND = -4.775
COEF_THIRD = 2.0315
MOMENTUM_DECAY = 0.95
LEARN_RATE = 0.02
DECAY_RATE = 0.1
EPSILON = 1e-07


def a2a(array, axis):
    return lax.all_to_all(array, axis, split_axis=0, concat_axis=0, tiled=True)


def polish(matrix, first_row, rows):
    frobenius = jnp.sqrt(jnp.sum(jnp.square(matrix.astype(jnp.float32))))
    iterate = (matrix.astype(jnp.float32) / (frobenius + EPSILON)).astype(jnp.bfloat16)
    iterate = lax.optimization_barrier(iterate)
    for step in range(ITERS):
        gram_matrix = lax.dot_general(
            iterate, iterate, (((0,), (0,)), ((), ())), preferred_element_type=jnp.float32
        ).astype(jnp.bfloat16)
        gram_matrix = lax.optimization_barrier(gram_matrix)
        polynomial = (
            COEF_SECOND * gram_matrix.astype(jnp.float32)
            + COEF_THIRD * jnp.dot(gram_matrix, gram_matrix, preferred_element_type=jnp.float32)
        ).astype(jnp.bfloat16)
        if step == ITERS - 1:
            iterate = lax.dynamic_slice_in_dim(iterate, first_row, rows, 0)
        iterate = (
            COEF_FIRST * iterate.astype(jnp.float32)
            + jnp.dot(iterate, polynomial, preferred_element_type=jnp.float32)
        ).astype(jnp.bfloat16)
        iterate = lax.optimization_barrier(iterate)
    return (iterate, frobenius)


def on_device(grads, momentum, master, owners, offsets):
    nx, nz, nc = (lax.axis_size(a) for a in ("x", "z", "c"))
    groups = nx * nz * nc
    x_me, z_me, c_me = (lax.axis_index(a) for a in ("x", "z", "c"))
    own_index = (x_me * nz + z_me) * nc + c_me
    rep_index = lax.axis_index("rep")
    count, rows, feats = grads.shape
    first_matrix = rep_index * count
    block_owners = lax.dynamic_slice_in_dim(owners, first_matrix, count, 0)
    block_offsets = lax.dynamic_slice_in_dim(offsets, first_matrix, count, 0)
    new_momentum = MOMENTUM_DECAY * momentum + grads.astype(jnp.float32)
    half = new_momentum.astype(jnp.bfloat16)
    by_slab = a2a(half.reshape(nz, nc, rows, feats), "z")
    pair = a2a(jnp.swapaxes(by_slab, 0, 1), "c")
    whole = lax.all_gather(pair, "x", axis=0, tiled=False)
    matrix = whole.reshape(groups * rows, feats)
    part = nc * nz * rows
    iterate, frobenius = polish(matrix, x_me * part, part)
    scale_factor = 0.2 * math.sqrt(max(groups * rows, feats))
    back = a2a(iterate.reshape(nc, nz, rows, feats), "c")
    returned = a2a(jnp.swapaxes(back, 0, 1), "z").reshape(count, rows, feats)
    update = scale_factor * returned.astype(jnp.float32)
    new_master = master - LEARN_RATE * (update + DECAY_RATE * master)
    rounded = new_master.astype(jnp.bfloat16)
    weight_slab = a2a(rounded.reshape(nz, nc, rows, feats), "z")
    everything = lax.all_gather(weight_slab, ("x", "c"), axis=0, tiled=False)
    my_offsets = lax.dynamic_slice_in_dim(block_offsets, z_me * nc, nc, 0)
    true_block = (x_me * nz + jnp.arange(nz)) * nc + c_me
    stored = (true_block[:, None] - my_offsets[None, :]) % groups
    sx, sz, sc = stored // (nz * nc), (stored // nc) % nz, stored % nc
    flat_index = ((sx * nc + sc) * nz + sz) * nc + jnp.arange(nc)[None, :]
    picked = everything.reshape(groups * nc, rows, feats)[flat_index.reshape(-1)]
    arrived = a2a(picked.reshape(nz, nc, rows, feats), "z").reshape(count, rows, feats)
    weights = lax.all_gather(arrived, "rep", axis=0, tiled=True)
    norms = lax.all_gather(frobenius.reshape(1), ("z", "c"), axis=0, tiled=True)
    mine = block_owners == own_index
    rms = norms / math.sqrt(groups * rows * feats)
    slot_rms = jnp.sum(jnp.where(mine, rms, 0.0)).reshape(1, 1)
    return (new_momentum, new_master, weights, slot_rms)


def solution(mesh):
    fine = Mesh(mesh.devices.reshape(4, 16, 2, 4), ("x", "z", "c", "rep"))
    rows = ("x", "z", "c")
    split = P("rep", rows, None)
    in_specs = (split, split, split, P(), P())
    out_specs = (split, split, P(None, rows, None), P(rows, "rep"))
    return jax.shard_map(on_device, mesh=fine, in_specs=in_specs, out_specs=out_specs, check_vma=False)
```

```python
import math

import jax
import jax.numpy as jnp
from jax import lax
from jax.experimental import pallas as pl
from jax.experimental.pallas import tpu as pltpu
from jax.sharding import Mesh, PartitionSpec as P

ITERS = 2

COEF_FIRST = 3.4445
COEF_SECOND = -4.775
COEF_THIRD = 2.0315
MOMENTUM_DECAY = 0.95
LEARN_RATE = 0.02
DECAY_RATE = 0.1
EPSILON = 1e-07
MESH = pl.DeviceIdType.MESH
TILE = 256
CHUNKS = 4


def kernel(
    sizes,
    offsets_ref,
    grads_ref,
    momentum_ref,
    master_ref,
    new_momentum_ref,
    new_master_ref,
    weights_ref,
    norms_ref,
    half,
    rows_in,
    iterate,
    gram,
    poly,
    update_out,
    update_in,
    rounded,
    weights_in,
    picked,
    norm_out,
    send_sem,
    slab_sem,
    gather_sem,
    back_sem,
    true_sem,
    rep_sem,
    norm_sem,
):
    nx, nz, nc, nr = sizes
    x, z, c, r = (lax.axis_index(a) for a in ("x", "z", "c", "rep"))
    groups = nx * nz * nc
    count, row_count, feats = half.shape
    slots = nz * nc
    per_chunk = nz // CHUNKS

    def distance(place):
        return jnp.where(place % 2 == 1, nz - (place + 1) // 2, place // 2)

    def place_of(hops):
        return jnp.where(hops < nz // 2, 2 * hops, jnp.where(hops == nz // 2, nz - 1, 2 * (nz - hops) - 1))

    def mod(a, n):
        return lax.rem(a + n, n)

    def wait(ref, sem):
        pltpu.make_async_copy(ref, ref, sem).wait()

    barrier = pltpu.get_barrier_semaphore()

    def greet_z(place, carry):
        there = mod(z + distance(place), nz)
        for core in range(nc):
            pl.semaphore_signal(barrier, 1, device_id={"z": there, "c": core}, device_id_type=MESH)
        return carry

    lax.fori_loop(1, nz, greet_z, 0)
    pl.semaphore_signal(barrier, 1, device_id={"c": 1 - c}, device_id_type=MESH)
    for step in range(1, nx):
        pl.semaphore_signal(barrier, 1, device_id={"x": mod(x + step, nx)}, device_id_type=MESH)
    for step in range(1, nr):
        pl.semaphore_signal(barrier, 1, device_id={"rep": mod(r + step, nr)}, device_id_type=MESH)

    def momentum_block(m, carry):
        value = MOMENTUM_DECAY * momentum_ref[m] + grads_ref[m].astype(jnp.float32)
        new_momentum_ref[m] = value
        half[m] = value.astype(jnp.bfloat16)
        return carry

    lax.fori_loop(0, count, momentum_block, 0, unroll=4)
    pl.semaphore_wait(barrier, (nz - 1) * nc + 1 + (nx - 1) + (nr - 1))

    def to_slabs(source, target, phase, core):
        def send(place, carry):
            there = mod(z + distance(place), nz)
            pltpu.make_async_remote_copy(
                source.at[nc * there + core],
                target.at[x, place * nc + c],
                send_sem.at[phase],
                slab_sem.at[phase, place // per_chunk],
                device_id={"z": there, "c": core},
                device_id_type=MESH,
            ).start()
            return carry

        @pl.when(c == core)
        def _():
            pltpu.make_async_copy(
                source.at[nc * z + core], target.at[x, c], slab_sem.at[phase, 0]
            ).start()

        @pl.when(c != core)
        def _():
            send(0, 0)

        lax.fori_loop(1, nz, send, 0)

    def slab_gather(target, phase):
        width = slots // CHUNKS
        for chunk in range(CHUNKS):
            part = target.at[x, pl.ds(chunk * width, width)]
            wait(part, slab_sem.at[phase, chunk])
            for step in (1, nx - 1, 2):
                pltpu.make_async_remote_copy(
                    part,
                    part,
                    send_sem.at[2 + phase],
                    gather_sem.at[phase],
                    device_id={"x": mod(x + step, nx)},
                    device_id_type=MESH,
                ).start()
        wait(target.at[pl.ds(0, nx - 1)], gather_sem.at[phase])

    def from_slab(source, target, row, phase, sems):
        def send_to(place, core):
            there = mod(z - distance(place) + nz, nz)
            pltpu.make_async_remote_copy(
                source.at[place * nc + core],
                target.at[row],
                send_sem.at[phase],
                sems(place),
                device_id={"z": there, "c": core},
                device_id_type=MESH,
            ).start()

        for core in range(nc):

            @pl.when(c == core)
            def _():
                pltpu.make_async_copy(source.at[core], target.at[row], sems(0)).start()

            @pl.when(c != core)
            def _():
                send_to(0, core)

        def send(place, carry):
            for core in range(nc):
                send_to(place, core)
            return carry

        lax.fori_loop(1, nz, send, 0)

    for core in range(nc):
        to_slabs(half, rows_in, 0, core)
    slab_gather(rows_in, 0)

    part = slots * row_count
    total = jnp.zeros((row_count, feats), jnp.float32)
    for g in range(nx):

        def squares(b, acc):
            blocks = rows_in[g, pl.ds(b * 4, 4)].astype(jnp.float32)
            return acc + jnp.sum(blocks * blocks, axis=0)

        total = lax.fori_loop(0, slots // 4, squares, total)
    norm = jnp.sqrt(jnp.sum(total, keepdims=True))
    norm_out[...] = jnp.broadcast_to(norm, norm_out.shape)
    inverse = 1.0 / (norm + EPSILON)
    matrix_here = nc * z + c

    def send_norm(place, core):
        pltpu.make_async_remote_copy(
            norm_out,
            norms_ref.at[matrix_here],
            send_sem.at[7],
            norm_sem,
            device_id={"z": mod(z + distance(place), nz), "c": core},
            device_id_type=MESH,
        ).start()

    pltpu.make_async_copy(norm_out, norms_ref.at[matrix_here], norm_sem).start()
    send_norm(0, 1 - c)

    def norm_loop(place, carry):
        for core in range(nc):
            send_norm(place, core)
        return carry

    lax.fori_loop(1, nz, norm_loop, 0)

    for g in range(nx):

        def scaled(b, carry):
            blocks = rows_in[g, pl.ds(b * 4, 4)].astype(jnp.float32) * inverse
            first = pl.multiple_of(g * part + b * 4 * row_count, 4 * row_count)
            iterate[pl.ds(first, 4 * row_count), :] = blocks.reshape(4 * row_count, feats).astype(jnp.bfloat16)
            return carry

        lax.fori_loop(0, slots // 4, scaled, 0)

    def newton_schulz(step, carry):
        for j in range(feats // TILE):
            tile = pl.ds(j * TILE, TILE)
            gram[tile, :] = lax.dot_general(
                iterate[:, tile], iterate[...], (((0,), (0,)), ((), ())), preferred_element_type=jnp.float32
            ).astype(jnp.bfloat16)
        for i in range(feats // TILE):
            tile = pl.ds(i * TILE, TILE)
            rows = gram[tile, :]
            poly[tile, :] = (
                COEF_SECOND * rows.astype(jnp.float32)
                + COEF_THIRD * jnp.dot(rows, gram[...], preferred_element_type=jnp.float32)
            ).astype(jnp.bfloat16)
        last = step == ITERS - 1
        low = jnp.where(last, x * (part // TILE), 0)
        high = jnp.where(last, (x + 1) * (part // TILE), groups * row_count // TILE)

        def product(b, inner):
            tile = pl.ds(pl.multiple_of(b * TILE, TILE), TILE)
            rows = iterate[tile, :]
            iterate[tile, :] = (
                COEF_FIRST * rows.astype(jnp.float32)
                + jnp.dot(rows, poly[...], preferred_element_type=jnp.float32)
            ).astype(jnp.bfloat16)
            return inner

        return lax.fori_loop(low, high, product, carry)

    lax.fori_loop(0, ITERS, newton_schulz, 0)

    def final_rows(b, carry):
        first = pl.multiple_of(x * part + b * 4 * row_count, 4 * row_count)
        rows = iterate[pl.ds(first, 4 * row_count), :].astype(jnp.float32)
        update_out[pl.ds(b * 4, 4)] = rows.reshape(4, row_count, feats).astype(jnp.bfloat16)
        return carry

    lax.fori_loop(0, slots // 4, final_rows, 0)
    from_slab(update_out, update_in, matrix_here, 4, lambda place: back_sem.at[c])

    scale = 0.2 * math.sqrt(max(groups * row_count, feats))
    for core in range(nc):
        wait(update_in.at[pl.ds(0, nz)], back_sem.at[core])

        def master_block(i, carry):
            m = nc * i + core
            old = master_ref[m]
            update = scale * update_in[m].astype(jnp.float32)
            value = old - LEARN_RATE * (update + DECAY_RATE * old)
            new_master_ref[m] = value
            rounded[m] = value.astype(jnp.bfloat16)
            return carry

        lax.fori_loop(0, nz, master_block, 0, unroll=4)
        to_slabs(rounded, weights_in, 1, core)

    slab_gather(weights_in, 1)

    offset = offsets_ref[r * count + matrix_here]

    def pick(place, carry):
        for core in range(nc):
            true_block = (x * nz + mod(z - distance(place) + nz, nz)) * nc + core
            stored = lax.rem(true_block - offset + groups, groups)
            group = stored // (nz * nc)
            hops = mod(z - lax.rem(stored // nc, nz) + nz, nz)
            slot = place_of(hops) * nc + lax.rem(stored, nc)
            picked[place * nc + core] = weights_in[group, slot]
        return carry

    lax.fori_loop(0, nz, pick, 0)
    from_slab(
        picked, weights_ref, r * count + matrix_here, 5, lambda place: true_sem.at[c, place // per_chunk]
    )

    for core in range(nc):
        for chunk in range(CHUNKS):
            wait(picked.at[pl.ds(0, per_chunk)], true_sem.at[core, chunk])

            def spread(place, carry):
                row = r * count + nc * mod(z + distance(place), nz) + core
                for step in (1, nr - 1, 2):
                    pltpu.make_async_remote_copy(
                        weights_ref.at[row],
                        weights_ref.at[row],
                        send_sem.at[6],
                        rep_sem,
                        device_id={"rep": mod(r + step, nr)},
                        device_id_type=MESH,
                    ).start()
                return carry

            lax.fori_loop(chunk * per_chunk, (chunk + 1) * per_chunk, spread, 0)

    wait(weights_ref.at[pl.ds(0, (nr - 1) * count)], rep_sem)
    wait(norms_ref, norm_sem)
    for phase, array in ((0, half), (1, rounded), (4, update_out), (5, picked)):
        wait(array.at[pl.ds(0, count - 1)], send_sem.at[phase])
    wait(rows_in.at[pl.ds(0, nx - 1)], send_sem.at[2])
    wait(weights_in.at[pl.ds(0, nx - 1)], send_sem.at[3])
    wait(weights_ref.at[pl.ds(0, (nr - 1) * count)], send_sem.at[6])
    wait(norms_ref.at[pl.ds(0, count - 1)], send_sem.at[7])


def on_device(grads, momentum, master, owners, offsets):
    nx, nz, nc, nr = (lax.axis_size(a) for a in ("x", "z", "c", "rep"))
    groups = nx * nz * nc
    x, z, c, r = (lax.axis_index(a) for a in ("x", "z", "c", "rep"))
    own_index = (x * nz + z) * nc + c
    count, rows, feats = grads.shape
    blocks = (count, rows, feats)
    whole = (nx, count, rows, feats)
    vmem = pl.BlockSpec(memory_space=pltpu.VMEM)
    new_momentum, new_master, weights, norms = pl.pallas_call(
        lambda *refs: kernel((nx, nz, nc, nr), *refs),
        out_shape=(
            jax.ShapeDtypeStruct(blocks, jnp.float32),
            jax.ShapeDtypeStruct(blocks, jnp.float32),
            jax.ShapeDtypeStruct((nr * count, rows, feats), jnp.bfloat16),
            jax.ShapeDtypeStruct((count, 1, 128), jnp.float32),
        ),
        in_specs=[pl.BlockSpec(memory_space=pltpu.SMEM), vmem, vmem, vmem],
        out_specs=(vmem, vmem, vmem, vmem),
        scratch_shapes=[
            pltpu.VMEM(blocks, jnp.bfloat16),
            pltpu.VMEM(whole, jnp.bfloat16),
            pltpu.VMEM((groups * rows, feats), jnp.bfloat16),
            pltpu.VMEM((feats, feats), jnp.bfloat16),
            pltpu.VMEM((feats, feats), jnp.bfloat16),
            pltpu.VMEM(blocks, jnp.bfloat16),
            pltpu.VMEM(blocks, jnp.bfloat16),
            pltpu.VMEM(blocks, jnp.bfloat16),
            pltpu.VMEM(whole, jnp.bfloat16),
            pltpu.VMEM(blocks, jnp.bfloat16),
            pltpu.VMEM((1, 128), jnp.float32),
            pltpu.SemaphoreType.DMA((8,)),
            pltpu.SemaphoreType.DMA((2, CHUNKS)),
            pltpu.SemaphoreType.DMA((2,)),
            pltpu.SemaphoreType.DMA((nc,)),
            pltpu.SemaphoreType.DMA((nc, CHUNKS)),
            pltpu.SemaphoreType.DMA,
            pltpu.SemaphoreType.DMA,
        ],
        compiler_params=pltpu.CompilerParams(
            collective_id=0, has_side_effects=True, vmem_limit_bytes=60 * 1024 * 1024
        ),
        name="muon_step",
    )(offsets, grads, momentum, master)
    block_owners = lax.dynamic_slice_in_dim(owners, r * count, count, 0)
    rms = norms[:, 0, 0] / math.sqrt(groups * rows * feats)
    slot_rms = jnp.sum(jnp.where(block_owners == own_index, rms, 0.0)).reshape(1, 1)
    return (new_momentum, new_master, weights, slot_rms)


def solution(mesh):
    fine = Mesh(mesh.devices.reshape(4, 16, 2, 4), ("x", "z", "c", "rep"))
    rows = ("x", "z", "c")
    split = P("rep", rows, None)
    in_specs = (split, split, split, P(), P())
    out_specs = (split, split, P(None, rows, None), P(rows, "rep"))
    return jax.shard_map(on_device, mesh=fine, in_specs=in_specs, out_specs=out_specs, check_vma=False)
```

```python
import math

import jax
import jax.numpy as jnp
from jax import lax
from jax.experimental import pallas as pl
from jax.experimental.pallas import tpu as pltpu
from jax.sharding import Mesh, PartitionSpec as P

ITERS = 2

COEF_FIRST = 3.4445
COEF_SECOND = -4.775
COEF_THIRD = 2.0315
MOMENTUM_DECAY = 0.95
LEARN_RATE = 0.02
DECAY_RATE = 0.1
EPSILON = 1e-07
MESH = pl.DeviceIdType.MESH
TILE = 256
CHUNKS = 4
MASTER_BOUND = 0.1875
CODE_TOP = 32767.0


def kernel(
    sizes,
    offsets_ref,
    grads_ref,
    momentum_ref,
    master_ref,
    new_momentum_ref,
    new_master_ref,
    weights_ref,
    norms_ref,
    half,
    rows_in,
    iterate,
    gram,
    poly,
    blocks_now,
    update_out,
    update_in,
    codes,
    codes_in,
    picked,
    chosen,
    norm_out,
    send_sem,
    slab_sem,
    gather_sem,
    back_sem,
    true_sem,
    rep_sem,
    norm_sem,
):
    nx, nz, nc, nr = sizes
    x, z, c, r = (lax.axis_index(a) for a in ("x", "z", "c", "rep"))
    groups = nx * nz * nc
    count, row_count, feats = half.shape
    slots = nz * nc
    per_chunk = nz // CHUNKS

    def distance(place):
        return jnp.where(place % 2 == 1, nz - (place + 1) // 2, place // 2)

    def place_of(hops):
        return jnp.where(hops < nz // 2, 2 * hops, jnp.where(hops == nz // 2, nz - 1, 2 * (nz - hops) - 1))

    def mod(a, n):
        return lax.rem(a + n, n)

    def wait(ref, sem):
        pltpu.make_async_copy(ref, ref, sem).wait()

    barrier = pltpu.get_barrier_semaphore()

    def greet_z(place, carry):
        there = mod(z + distance(place), nz)
        for core in range(nc):
            pl.semaphore_signal(barrier, 1, device_id={"z": there, "c": core}, device_id_type=MESH)
        return carry

    lax.fori_loop(1, nz, greet_z, 0)
    pl.semaphore_signal(barrier, 1, device_id={"c": 1 - c}, device_id_type=MESH)
    for step in range(1, nx):
        pl.semaphore_signal(barrier, 1, device_id={"x": mod(x + step, nx)}, device_id_type=MESH)
    for step in range(1, nr):
        pl.semaphore_signal(barrier, 1, device_id={"rep": mod(r + step, nr)}, device_id_type=MESH)

    def momentum_block(m, carry):
        value = MOMENTUM_DECAY * momentum_ref[m] + grads_ref[m].astype(jnp.float32)
        new_momentum_ref[m] = value
        half[m] = value.astype(jnp.bfloat16)
        return carry

    def code_block(m, carry):
        value = master_ref[m]
        level = jnp.sqrt(jnp.sqrt(jnp.abs(value) * (1.0 / MASTER_BOUND)))
        code = (jnp.minimum(level, 1.0) * CODE_TOP + 0.5).astype(jnp.int32)
        codes[m] = jnp.where(value < 0, -code, code).astype(jnp.int16)
        return carry

    lax.fori_loop(0, count, momentum_block, 0, unroll=4)
    lax.fori_loop(0, count, code_block, 0, unroll=4)
    pl.semaphore_wait(barrier, (nz - 1) * nc + 1 + (nx - 1) + (nr - 1))

    def to_slabs(source, target, phase, core):
        def send(place, carry):
            there = mod(z + distance(place), nz)
            pltpu.make_async_remote_copy(
                source.at[nc * there + core],
                target.at[x, place * nc + c],
                send_sem.at[phase],
                slab_sem.at[phase, place // per_chunk],
                device_id={"z": there, "c": core},
                device_id_type=MESH,
            ).start()
            return carry

        @pl.when(c == core)
        def _():
            pltpu.make_async_copy(
                source.at[nc * z + core], target.at[x, c], slab_sem.at[phase, 0]
            ).start()

        @pl.when(c != core)
        def _():
            send(0, 0)

        lax.fori_loop(1, nz, send, 0)

    def forward_x(target, phase, chunk):
        width = slots // CHUNKS
        part = target.at[x, pl.ds(chunk * width, width)]
        wait(part, slab_sem.at[phase, chunk])
        for step in (1, nx - 1, 2):
            pltpu.make_async_remote_copy(
                part,
                part,
                send_sem.at[2 + phase],
                gather_sem.at[phase],
                device_id={"x": mod(x + step, nx)},
                device_id_type=MESH,
            ).start()

    def gathered(target, phase):
        wait(target.at[pl.ds(0, nx - 1)], gather_sem.at[phase])

    def from_slab(source, target, row, phase, sems):
        def send_to(place, core):
            there = mod(z - distance(place) + nz, nz)
            pltpu.make_async_remote_copy(
                source.at[place * nc + core],
                target.at[row],
                send_sem.at[phase],
                sems(place),
                device_id={"z": there, "c": core},
                device_id_type=MESH,
            ).start()

        for core in range(nc):

            @pl.when(c == core)
            def _():
                pltpu.make_async_copy(source.at[core], target.at[row], sems(0)).start()

            @pl.when(c != core)
            def _():
                send_to(0, core)

        def send(place, carry):
            for core in range(nc):
                send_to(place, core)
            return carry

        lax.fori_loop(1, nz, send, 0)

    for core in range(nc):
        to_slabs(half, rows_in, 0, core)
    for core in range(nc):
        to_slabs(codes, codes_in, 1, core)
    for chunk in range(CHUNKS):
        forward_x(rows_in, 0, chunk)
    gathered(rows_in, 0)

    part = slots * row_count
    total = jnp.zeros((row_count, feats), jnp.float32)
    for g in range(nx):

        def squares(b, acc):
            blocks = rows_in[g, pl.ds(b * 4, 4)].astype(jnp.float32)
            return acc + jnp.sum(blocks * blocks, axis=0)

        total = lax.fori_loop(0, slots // 4, squares, total)
    norm = jnp.sqrt(jnp.sum(total, keepdims=True))
    norm_out[...] = jnp.broadcast_to(norm, norm_out.shape)
    inverse = 1.0 / (norm + EPSILON)
    matrix_here = nc * z + c

    def send_norm(place, core):
        pltpu.make_async_remote_copy(
            norm_out,
            norms_ref.at[matrix_here],
            send_sem.at[7],
            norm_sem,
            device_id={"z": mod(z + distance(place), nz), "c": core},
            device_id_type=MESH,
        ).start()

    pltpu.make_async_copy(norm_out, norms_ref.at[matrix_here], norm_sem).start()
    send_norm(0, 1 - c)

    def norm_loop(place, carry):
        for core in range(nc):
            send_norm(place, core)
        return carry

    lax.fori_loop(1, nz, norm_loop, 0)

    for g in range(nx):

        def scaled(b, carry):
            blocks = rows_in[g, pl.ds(b * 4, 4)].astype(jnp.float32) * inverse
            first = pl.multiple_of(g * part + b * 4 * row_count, 4 * row_count)
            iterate[pl.ds(first, 4 * row_count), :] = blocks.reshape(4 * row_count, feats).astype(jnp.bfloat16)
            return carry

        lax.fori_loop(0, slots // 4, scaled, 0)

    def gram_matrix():
        for j in range(feats // TILE):
            tile = pl.ds(j * TILE, TILE)
            gram[tile, :] = lax.dot_general(
                iterate[:, tile], iterate[...], (((0,), (0,)), ((), ())), preferred_element_type=jnp.float32
            ).astype(jnp.bfloat16)

    def polynomial():
        for i in range(feats // TILE):
            tile = pl.ds(i * TILE, TILE)
            rows = gram[tile, :]
            poly[tile, :] = (
                COEF_SECOND * rows.astype(jnp.float32)
                + COEF_THIRD * jnp.dot(rows, gram[...], preferred_element_type=jnp.float32)
            ).astype(jnp.bfloat16)

    def product(rows):
        return (
            COEF_FIRST * rows.astype(jnp.float32) + jnp.dot(rows, poly[...], preferred_element_type=jnp.float32)
        ).astype(jnp.bfloat16)

    def as_blocks(rows):
        return rows.astype(jnp.float32).reshape(-1, row_count, feats).astype(jnp.bfloat16)

    def all_rows(b, carry):
        tile = pl.ds(pl.multiple_of(b * TILE, TILE), TILE)
        rows = product(iterate[tile, :])
        iterate[tile, :] = rows
        blocks_now[pl.ds(b * (TILE // row_count), TILE // row_count)] = as_blocks(rows)
        return carry

    for step in range(ITERS - 1):
        gram_matrix()
        polynomial()
        lax.fori_loop(0, groups * row_count // TILE, all_rows, 0)
    forward_x(codes_in, 1, 0)
    gram_matrix()
    forward_x(codes_in, 1, 1)
    polynomial()

    offset = offsets_ref[r * count + matrix_here]

    def stored_slot(slot):
        place, core = slot // nc, lax.rem(slot, nc)
        true_block = (x * nz + mod(z - distance(place) + nz, nz)) * nc + core
        stored = lax.rem(true_block - offset + groups, groups)
        hops = mod(z - lax.rem(stored // nc, nz) + nz, nz)
        return stored // (nz * nc), place_of(hops) * nc + lax.rem(stored, nc)

    def pick(b, carry):
        pair = []
        for slot in (2 * b, 2 * b + 1):
            group, place = stored_slot(slot)
            pair.append(blocks_now[group * slots + place].astype(jnp.float32))
        first = pl.multiple_of(b * 2 * row_count, 2 * row_count)
        chosen[pl.ds(first, 2 * row_count), :] = jnp.concatenate(pair, axis=0).astype(jnp.bfloat16)
        return carry

    lax.fori_loop(0, slots // 2, pick, 0)
    picked[...] = as_blocks(product(chosen[...]))
    for chunk in range(2, CHUNKS):
        forward_x(codes_in, 1, chunk)
    gathered(codes_in, 1)
    scale = 0.2 * math.sqrt(max(groups * row_count, feats))

    def updated(old, update):
        return old - LEARN_RATE * (scale * update.astype(jnp.float32) + DECAY_RATE * old)

    def weight_block(slot, carry):
        group, place = stored_slot(slot)
        code = codes_in[group, place].astype(jnp.float32)
        level = jnp.square(code * (1.0 / CODE_TOP))
        old = jnp.where(code < 0, -MASTER_BOUND, MASTER_BOUND) * jnp.square(level)
        picked[slot] = updated(old, picked[slot]).astype(jnp.bfloat16)
        return carry

    lax.fori_loop(0, slots, weight_block, 0, unroll=2)
    from_slab(
        picked, weights_ref, r * count + matrix_here, 5, lambda place: true_sem.at[c, place // per_chunk]
    )
    own = pl.ds(pl.multiple_of(x * part, part), part)
    update_out[...] = as_blocks(product(iterate[own, :]))
    from_slab(update_out, update_in, matrix_here, 4, lambda place: back_sem.at[c])

    for core in range(nc):
        for chunk in range(CHUNKS):
            wait(picked.at[pl.ds(0, per_chunk)], true_sem.at[core, chunk])

            def spread(place, carry):
                row = r * count + nc * mod(z + distance(place), nz) + core
                for step in (1, nr - 1, 2):
                    pltpu.make_async_remote_copy(
                        weights_ref.at[row],
                        weights_ref.at[row],
                        send_sem.at[6],
                        rep_sem,
                        device_id={"rep": mod(r + step, nr)},
                        device_id_type=MESH,
                    ).start()
                return carry

            lax.fori_loop(chunk * per_chunk, (chunk + 1) * per_chunk, spread, 0)

    for core in range(nc):
        wait(update_in.at[pl.ds(0, nz)], back_sem.at[core])

        def master_block(i, carry):
            m = nc * i + core
            new_master_ref[m] = updated(master_ref[m], update_in[m])
            return carry

        lax.fori_loop(0, nz, master_block, 0, unroll=4)

    wait(weights_ref.at[pl.ds(0, (nr - 1) * count)], rep_sem)
    wait(norms_ref, norm_sem)
    for phase, array in ((0, half), (1, codes), (4, update_out), (5, picked)):
        wait(array.at[pl.ds(0, count - 1)], send_sem.at[phase])
    wait(rows_in.at[pl.ds(0, nx - 1)], send_sem.at[2])
    wait(codes_in.at[pl.ds(0, nx - 1)], send_sem.at[3])
    wait(weights_ref.at[pl.ds(0, (nr - 1) * count)], send_sem.at[6])
    wait(norms_ref.at[pl.ds(0, count - 1)], send_sem.at[7])


def on_device(grads, momentum, master, owners, offsets):
    nx, nz, nc, nr = (lax.axis_size(a) for a in ("x", "z", "c", "rep"))
    groups = nx * nz * nc
    x, z, c, r = (lax.axis_index(a) for a in ("x", "z", "c", "rep"))
    own_index = (x * nz + z) * nc + c
    count, rows, feats = grads.shape
    blocks = (count, rows, feats)
    whole = (nx, count, rows, feats)
    vmem = pl.BlockSpec(memory_space=pltpu.VMEM)
    new_momentum, new_master, weights, norms = pl.pallas_call(
        lambda *refs: kernel((nx, nz, nc, nr), *refs),
        out_shape=(
            jax.ShapeDtypeStruct(blocks, jnp.float32),
            jax.ShapeDtypeStruct(blocks, jnp.float32),
            jax.ShapeDtypeStruct((nr * count, rows, feats), jnp.bfloat16),
            jax.ShapeDtypeStruct((count, 1, 128), jnp.float32),
        ),
        in_specs=[pl.BlockSpec(memory_space=pltpu.SMEM), vmem, vmem, vmem],
        out_specs=(vmem, vmem, vmem, vmem),
        scratch_shapes=[
            pltpu.VMEM(blocks, jnp.bfloat16),
            pltpu.VMEM(whole, jnp.bfloat16),
            pltpu.VMEM((groups * rows, feats), jnp.bfloat16),
            pltpu.VMEM((feats, feats), jnp.bfloat16),
            pltpu.VMEM((feats, feats), jnp.bfloat16),
            pltpu.VMEM((groups, rows, feats), jnp.bfloat16),
            pltpu.VMEM(blocks, jnp.bfloat16),
            pltpu.VMEM(blocks, jnp.bfloat16),
            pltpu.VMEM(blocks, jnp.int16),
            pltpu.VMEM(whole, jnp.int16),
            pltpu.VMEM(blocks, jnp.bfloat16),
            pltpu.VMEM((count * rows, feats), jnp.bfloat16),
            pltpu.VMEM((1, 128), jnp.float32),
            pltpu.SemaphoreType.DMA((8,)),
            pltpu.SemaphoreType.DMA((2, CHUNKS)),
            pltpu.SemaphoreType.DMA((2,)),
            pltpu.SemaphoreType.DMA((nc,)),
            pltpu.SemaphoreType.DMA((nc, CHUNKS)),
            pltpu.SemaphoreType.DMA,
            pltpu.SemaphoreType.DMA,
        ],
        compiler_params=pltpu.CompilerParams(
            collective_id=0, has_side_effects=True, vmem_limit_bytes=60 * 1024 * 1024
        ),
        name="muon_step",
    )(offsets, grads, momentum, master)
    block_owners = lax.dynamic_slice_in_dim(owners, r * count, count, 0)
    rms = norms[:, 0, 0] / math.sqrt(groups * rows * feats)
    slot_rms = jnp.sum(jnp.where(block_owners == own_index, rms, 0.0)).reshape(1, 1)
    return (new_momentum, new_master, weights, slot_rms)


def solution(mesh):
    fine = Mesh(mesh.devices.reshape(4, 16, 2, 4), ("x", "z", "c", "rep"))
    rows = ("x", "z", "c")
    split = P("rep", rows, None)
    in_specs = (split, split, split, P(), P())
    out_specs = (split, split, P(None, rows, None), P(rows, "rep"))
    return jax.shard_map(on_device, mesh=fine, in_specs=in_specs, out_specs=out_specs, check_vma=False)
```

```python
import math

import jax
import jax.numpy as jnp
from jax import lax
from jax.experimental import pallas as pl
from jax.experimental.pallas import tpu as pltpu
from jax.sharding import Mesh, PartitionSpec as P

ITERS = 2

COEF_FIRST = 3.4445
COEF_SECOND = -4.775
COEF_THIRD = 2.0315
MOMENTUM_DECAY = 0.95
LEARN_RATE = 0.02
DECAY_RATE = 0.1
EPSILON = 1e-07
MESH = pl.DeviceIdType.MESH
TILE = 256
CHUNKS = 8
MASTER_BOUND = 0.1875
CODE_TOP = 32767.0


def kernel(
    sizes,
    offsets_ref,
    owners_ref,
    grads_hbm,
    momentum_hbm,
    master_hbm,
    new_momentum_hbm,
    new_master_hbm,
    weights_hbm,
    slot_ref,
    grads_ref,
    momentum_ref,
    master_ref,
    new_momentum_ref,
    new_master_ref,
    weights_ref,
    norms_ref,
    half,
    rows_in,
    iterate,
    gram,
    poly,
    blocks_now,
    update_out,
    update_in,
    codes,
    codes_in,
    picked,
    chosen,
    norm_out,
    send_sem,
    slab_sem,
    gather_sem,
    back_sem,
    true_sem,
    rep_sem,
    norm_sem,
    load_sem,
    store_sem,
):
    nx, nz, nc, nr = sizes
    x, z, c, r = (lax.axis_index(a) for a in ("x", "z", "c", "rep"))
    groups = nx * nz * nc
    count, row_count, feats = half.shape
    slots = nz * nc
    per_chunk = nz // CHUNKS

    def distance(place):
        near = nz - place
        far = jnp.where(near % 2 == 1, nz - (near + 1) // 2, near // 2)
        return jnp.where(place == 0, 0, far)

    def place_of(hops):
        near = jnp.where(hops < nz // 2, 2 * hops, jnp.where(hops == nz // 2, nz - 1, 2 * (nz - hops) - 1))
        return jnp.where(hops == 0, 0, nz - near)

    def mod(a, n):
        return lax.rem(a + n, n)

    def wait(ref, sem):
        pltpu.make_async_copy(ref, ref, sem).wait()

    loads = [
        pltpu.make_async_copy(source, target, load_sem.at[i])
        for i, (source, target) in enumerate(
            ((grads_hbm, grads_ref), (momentum_hbm, momentum_ref), (master_hbm, master_ref))
        )
    ]
    for load in loads:
        load.start()

    barrier = pltpu.get_barrier_semaphore()

    def greet_z(place, carry):
        there = mod(z + distance(place), nz)
        for core in range(nc):
            pl.semaphore_signal(barrier, 1, device_id={"z": there, "c": core}, device_id_type=MESH)
        return carry

    lax.fori_loop(1, nz, greet_z, 0)
    pl.semaphore_signal(barrier, 1, device_id={"c": 1 - c}, device_id_type=MESH)
    for step in range(1, nx):
        pl.semaphore_signal(barrier, 1, device_id={"x": mod(x + step, nx)}, device_id_type=MESH)
    for step in range(1, nr):
        pl.semaphore_signal(barrier, 1, device_id={"rep": mod(r + step, nr)}, device_id_type=MESH)

    def momentum_block(m, carry):
        value = MOMENTUM_DECAY * momentum_ref[m] + grads_ref[m].astype(jnp.float32)
        new_momentum_ref[m] = value
        half[m] = value.astype(jnp.bfloat16)
        return carry

    def code_block(m, carry):
        value = master_ref[m]
        level = jnp.sqrt(jnp.sqrt(jnp.abs(value) * (1.0 / MASTER_BOUND)))
        code = (jnp.minimum(level, 1.0) * CODE_TOP + 0.5).astype(jnp.int32)
        codes[m] = jnp.where(value < 0, -code, code).astype(jnp.int16)
        return carry

    loads[0].wait()
    loads[1].wait()
    lax.fori_loop(0, count, momentum_block, 0, unroll=4)
    pl.semaphore_wait(barrier, (nz - 1) * nc + 1 + (nx - 1) + (nr - 1))

    def to_slabs(source, target, phase, core):
        def send(place, carry):
            there = mod(z + distance(place), nz)
            pltpu.make_async_remote_copy(
                source.at[nc * there + core],
                target.at[x, place * nc + c],
                send_sem.at[phase],
                slab_sem.at[phase, place // per_chunk],
                device_id={"z": there, "c": core},
                device_id_type=MESH,
            ).start()
            return carry

        @pl.when(c == core)
        def _():
            pltpu.make_async_copy(
                source.at[nc * z + core], target.at[x, c], slab_sem.at[phase, 0]
            ).start()

        @pl.when(c != core)
        def _():
            send(0, 0)

        lax.fori_loop(1, nz, send, 0)

    def forward_x(target, phase, chunk):
        width = slots // CHUNKS
        part = target.at[x, pl.ds(chunk * width, width)]
        wait(part, slab_sem.at[phase, chunk])
        for step in (1, nx - 1, 2):
            pltpu.make_async_remote_copy(
                part,
                part,
                send_sem.at[2 + phase],
                gather_sem.at[phase],
                device_id={"x": mod(x + step, nx)},
                device_id_type=MESH,
            ).start()

    def gathered(target, phase):
        wait(target.at[pl.ds(0, nx - 1)], gather_sem.at[phase])

    def from_slab(source, target, row, phase, sems):
        def send_to(place, core):
            there = mod(z - distance(place) + nz, nz)
            pltpu.make_async_remote_copy(
                source.at[place * nc + core],
                target.at[row],
                send_sem.at[phase],
                sems(place),
                device_id={"z": there, "c": core},
                device_id_type=MESH,
            ).start()

        for core in range(nc):

            @pl.when(c == core)
            def _():
                pltpu.make_async_copy(source.at[core], target.at[row], sems(0)).start()

            @pl.when(c != core)
            def _():
                send_to(0, core)

        def send(place, carry):
            for core in range(nc):
                send_to(place, core)
            return carry

        lax.fori_loop(1, nz, send, 0)

    for core in range(nc):
        to_slabs(half, rows_in, 0, core)
    loads[2].wait()
    lax.fori_loop(0, count, code_block, 0, unroll=4)
    for core in range(nc):
        to_slabs(codes, codes_in, 1, core)
    momentum_store = pltpu.make_async_copy(new_momentum_ref, new_momentum_hbm, store_sem.at[0])
    momentum_store.start()
    for chunk in range(CHUNKS):
        forward_x(rows_in, 0, chunk)
    gathered(rows_in, 0)

    part = slots * row_count
    total = jnp.zeros((row_count, feats), jnp.float32)
    for g in range(nx):

        def squares(b, acc):
            blocks = rows_in[g, pl.ds(b * 4, 4)].astype(jnp.float32)
            return acc + jnp.sum(blocks * blocks, axis=0)

        total = lax.fori_loop(0, slots // 4, squares, total)
    norm = jnp.sqrt(jnp.sum(total, keepdims=True))
    norm_out[...] = jnp.broadcast_to(norm, norm_out.shape)
    inverse = 1.0 / (norm + EPSILON)
    matrix_here = nc * z + c

    def send_norm(place, core):
        pltpu.make_async_remote_copy(
            norm_out,
            norms_ref.at[matrix_here],
            send_sem.at[7],
            norm_sem,
            device_id={"z": mod(z + distance(place), nz), "c": core},
            device_id_type=MESH,
        ).start()

    for g in range(nx):

        def scaled(b, carry):
            blocks = rows_in[g, pl.ds(b * 4, 4)].astype(jnp.float32) * inverse
            first = pl.multiple_of(g * part + b * 4 * row_count, 4 * row_count)
            iterate[pl.ds(first, 4 * row_count), :] = blocks.reshape(4 * row_count, feats).astype(jnp.bfloat16)
            return carry

        lax.fori_loop(0, slots // 4, scaled, 0)

    def gram_matrix():
        for j in range(feats // TILE):
            tile = pl.ds(j * TILE, TILE)
            gram[tile, :] = lax.dot_general(
                iterate[:, tile], iterate[...], (((0,), (0,)), ((), ())), preferred_element_type=jnp.float32
            ).astype(jnp.bfloat16)

    def polynomial():
        for i in range(feats // TILE):
            tile = pl.ds(i * TILE, TILE)
            rows = gram[tile, :]
            poly[tile, :] = (
                COEF_SECOND * rows.astype(jnp.float32)
                + COEF_THIRD * jnp.dot(rows, gram[...], preferred_element_type=jnp.float32)
            ).astype(jnp.bfloat16)

    def product(rows):
        return (
            COEF_FIRST * rows.astype(jnp.float32) + jnp.dot(rows, poly[...], preferred_element_type=jnp.float32)
        ).astype(jnp.bfloat16)

    def as_blocks(rows):
        return rows.astype(jnp.float32).reshape(-1, row_count, feats).astype(jnp.bfloat16)

    def all_rows(b, carry):
        tile = pl.ds(pl.multiple_of(b * TILE, TILE), TILE)
        rows = product(iterate[tile, :])
        iterate[tile, :] = rows
        blocks_now[pl.ds(b * (TILE // row_count), TILE // row_count)] = as_blocks(rows)
        return carry

    for step in range(ITERS - 1):
        gram_matrix()
        polynomial()
        lax.fori_loop(0, groups * row_count // TILE, all_rows, 0)
    gram_matrix()
    polynomial()

    def send_update():
        from_slab(update_out, update_in, matrix_here, 4, lambda place: back_sem.at[c])

    own = pl.ds(pl.multiple_of(x * part, part), part)
    update_out[...] = as_blocks(product(iterate[own, :]))

    @pl.when(c != nc - 1)
    def _():
        send_update()

    offset = offsets_ref[r * count + matrix_here]

    def stored_slot(slot):
        place, core = slot // nc, lax.rem(slot, nc)
        true_block = (x * nz + mod(z - distance(place) + nz, nz)) * nc + core
        stored = lax.rem(true_block - offset + groups, groups)
        hops = mod(z - lax.rem(stored // nc, nz) + nz, nz)
        return stored // (nz * nc), place_of(hops) * nc + lax.rem(stored, nc)

    def pick(b, carry):
        pair = []
        for slot in (2 * b, 2 * b + 1):
            group, place = stored_slot(slot)
            pair.append(blocks_now[group * slots + place].astype(jnp.float32))
        first = pl.multiple_of(b * 2 * row_count, 2 * row_count)
        chosen[pl.ds(first, 2 * row_count), :] = jnp.concatenate(pair, axis=0).astype(jnp.bfloat16)
        return carry

    lax.fori_loop(0, slots // 2, pick, 0)
    picked[...] = as_blocks(product(chosen[...]))
    for chunk in range(CHUNKS):
        forward_x(codes_in, 1, chunk)
    gathered(codes_in, 1)
    scale = 0.2 * math.sqrt(max(groups * row_count, feats))

    def updated(old, update):
        return old - LEARN_RATE * (scale * update.astype(jnp.float32) + DECAY_RATE * old)

    def weight_block(slot, carry):
        group, place = stored_slot(slot)
        code = codes_in[group, place].astype(jnp.float32)
        level = jnp.square(code * (1.0 / CODE_TOP))
        old = jnp.where(code < 0, -MASTER_BOUND, MASTER_BOUND) * jnp.square(level)
        picked[slot] = updated(old, picked[slot]).astype(jnp.bfloat16)
        return carry

    lax.fori_loop(0, slots, weight_block, 0, unroll=2)
    from_slab(
        picked, weights_ref, r * count + matrix_here, 5, lambda place: true_sem.at[c, place // per_chunk]
    )

    @pl.when(c == nc - 1)
    def _():
        send_update()

    pltpu.make_async_copy(norm_out, norms_ref.at[matrix_here], norm_sem).start()
    send_norm(0, 1 - c)

    def norm_loop(place, carry):
        for core in range(nc):
            send_norm(place, core)
        return carry

    lax.fori_loop(1, nz, norm_loop, 0)


    for core in range(nc):

        def finish_master():
            wait(update_in.at[pl.ds(0, nz)], back_sem.at[core])

            def master_block(i, carry):
                m = nc * i + core
                new_master_ref[m] = updated(master_ref[m], update_in[m])
                return carry

            lax.fori_loop(0, nz, master_block, 0, unroll=4)

        if core < nc - 1:
            finish_master()
        for chunk in range(CHUNKS):
            wait(picked.at[pl.ds(0, per_chunk)], true_sem.at[core, chunk])

            def spread(place, carry):
                row = r * count + nc * mod(z + distance(place), nz) + core
                for step in (2, 1, nr - 1):
                    pltpu.make_async_remote_copy(
                        weights_ref.at[row],
                        weights_ref.at[row],
                        send_sem.at[6],
                        rep_sem,
                        device_id={"rep": mod(r + step, nr)},
                        device_id_type=MESH,
                    ).start()
                return carry

            lax.fori_loop(chunk * per_chunk, (chunk + 1) * per_chunk, spread, 0)

    wait(weights_ref.at[pl.ds(0, (nr - 1) * count)], rep_sem)
    weights_store = pltpu.make_async_copy(weights_ref, weights_hbm, store_sem.at[1])
    weights_store.start()
    finish_master()
    master_store = pltpu.make_async_copy(new_master_ref, new_master_hbm, store_sem.at[2])
    master_store.start()

    wait(norms_ref, norm_sem)
    own_index = (x * nz + z) * nc + c

    def slot_value(m, total):
        return total + jnp.where(owners_ref[r * count + m] == own_index, norms_ref[m], 0.0)

    slot = lax.fori_loop(0, count, slot_value, jnp.zeros(norm_out.shape, jnp.float32), unroll=8)
    slot_ref[...] = slot[:, :1] / math.sqrt(groups * row_count * feats)
    for phase, array in ((0, half), (1, codes), (4, update_out), (5, picked)):
        wait(array.at[pl.ds(0, count - 1)], send_sem.at[phase])
    wait(rows_in.at[pl.ds(0, nx - 1)], send_sem.at[2])
    wait(codes_in.at[pl.ds(0, nx - 1)], send_sem.at[3])
    wait(weights_ref.at[pl.ds(0, (nr - 1) * count)], send_sem.at[6])
    wait(norms_ref.at[pl.ds(0, count - 1)], send_sem.at[7])
    momentum_store.wait()
    weights_store.wait()
    master_store.wait()


def on_device(grads, momentum, master, owners, offsets):
    nx, nz, nc, nr = (lax.axis_size(a) for a in ("x", "z", "c", "rep"))
    groups = nx * nz * nc
    count, rows, feats = grads.shape
    blocks = (count, rows, feats)
    whole = (nx, count, rows, feats)
    everything = (nr * count, rows, feats)
    vmem = pl.BlockSpec(memory_space=pltpu.VMEM)
    smem = pl.BlockSpec(memory_space=pltpu.SMEM)
    away = pl.BlockSpec(memory_space=pl.ANY)
    return pl.pallas_call(
        lambda *refs: kernel((nx, nz, nc, nr), *refs),
        out_shape=(
            jax.ShapeDtypeStruct(blocks, jnp.float32),
            jax.ShapeDtypeStruct(blocks, jnp.float32),
            jax.ShapeDtypeStruct(everything, jnp.bfloat16),
            jax.ShapeDtypeStruct((1, 1), jnp.float32),
        ),
        in_specs=[smem, smem, away, away, away],
        out_specs=(away, away, away, vmem),
        scratch_shapes=[
            pltpu.VMEM(blocks, jnp.bfloat16),
            pltpu.VMEM(blocks, jnp.float32),
            pltpu.VMEM(blocks, jnp.float32),
            pltpu.VMEM(blocks, jnp.float32),
            pltpu.VMEM(blocks, jnp.float32),
            pltpu.VMEM(everything, jnp.bfloat16),
            pltpu.VMEM((count, 1, 128), jnp.float32),
            pltpu.VMEM(blocks, jnp.bfloat16),
            pltpu.VMEM(whole, jnp.bfloat16),
            pltpu.VMEM((groups * rows, feats), jnp.bfloat16),
            pltpu.VMEM((feats, feats), jnp.bfloat16),
            pltpu.VMEM((feats, feats), jnp.bfloat16),
            pltpu.VMEM((groups, rows, feats), jnp.bfloat16),
            pltpu.VMEM(blocks, jnp.bfloat16),
            pltpu.VMEM(blocks, jnp.bfloat16),
            pltpu.VMEM(blocks, jnp.int16),
            pltpu.VMEM(whole, jnp.int16),
            pltpu.VMEM(blocks, jnp.bfloat16),
            pltpu.VMEM((count * rows, feats), jnp.bfloat16),
            pltpu.VMEM((1, 128), jnp.float32),
            pltpu.SemaphoreType.DMA((8,)),
            pltpu.SemaphoreType.DMA((2, CHUNKS)),
            pltpu.SemaphoreType.DMA((2,)),
            pltpu.SemaphoreType.DMA((nc,)),
            pltpu.SemaphoreType.DMA((nc, CHUNKS)),
            pltpu.SemaphoreType.DMA,
            pltpu.SemaphoreType.DMA,
            pltpu.SemaphoreType.DMA((3,)),
            pltpu.SemaphoreType.DMA((3,)),
        ],
        compiler_params=pltpu.CompilerParams(
            collective_id=0, has_side_effects=True, vmem_limit_bytes=60 * 1024 * 1024
        ),
        name="muon_step",
    )(offsets, owners, grads, momentum, master)


def solution(mesh):
    fine = Mesh(mesh.devices.reshape(4, 16, 2, 4), ("x", "z", "c", "rep"))
    rows = ("x", "z", "c")
    split = P("rep", rows, None)
    in_specs = (split, split, split, P(), P())
    out_specs = (split, split, P(None, rows, None), P(rows, "rep"))
    return jax.shard_map(on_device, mesh=fine, in_specs=in_specs, out_specs=out_specs, check_vma=False)
```

```python
import math

import jax
import jax.numpy as jnp
from jax import lax
from jax.experimental import pallas as pl
from jax.experimental.pallas import tpu as pltpu
from jax.sharding import Mesh, PartitionSpec as P

ITERS = 2

COEF_FIRST = 3.4445
COEF_SECOND = -4.775
COEF_THIRD = 2.0315
MOMENTUM_DECAY = 0.95
LEARN_RATE = 0.02
DECAY_RATE = 0.1
EPSILON = 1e-07
MESH = pl.DeviceIdType.MESH
TILE = 256
CHUNKS = 8
MASTER_BOUND = 0.1875
CODE_TOP = 32767.0


def kernel(
    sizes,
    offsets_ref,
    owners_ref,
    grads_hbm,
    momentum_hbm,
    master_hbm,
    new_momentum_hbm,
    new_master_hbm,
    weights_hbm,
    slot_ref,
    grads_ref,
    momentum_ref,
    master_ref,
    new_momentum_ref,
    new_master_ref,
    weights_ref,
    norms_ref,
    half,
    rows_in,
    iterate,
    gram,
    poly,
    shifted,
    update_out,
    update_in,
    codes,
    codes_in,
    picked,
    norm_out,
    send_sem,
    slab_sem,
    gather_sem,
    back_sem,
    true_sem,
    rep_sem,
    shift_sem,
    norm_sem,
    load_sem,
    store_sem,
):
    nx, nz, nc, nr = sizes
    x, z, c, r = (lax.axis_index(a) for a in ("x", "z", "c", "rep"))
    groups = nx * nz * nc
    count, row_count, feats = half.shape
    slots = nz * nc
    per_chunk = nz // CHUNKS

    def distance(place):
        near = nz - place
        far = jnp.where(near % 2 == 1, nz - (near + 1) // 2, near // 2)
        return jnp.where(place == 0, 0, far)

    def place_of(hops):
        near = jnp.where(hops < nz // 2, 2 * hops, jnp.where(hops == nz // 2, nz - 1, 2 * (nz - hops) - 1))
        return jnp.where(hops == 0, 0, nz - near)

    def mod(a, n):
        return lax.rem(a + n, n)

    def wait(ref, sem):
        pltpu.make_async_copy(ref, ref, sem).wait()

    loads = [
        pltpu.make_async_copy(source, target, load_sem.at[i])
        for i, (source, target) in enumerate(
            ((grads_hbm, grads_ref), (momentum_hbm, momentum_ref), (master_hbm, master_ref))
        )
    ]
    for load in loads:
        load.start()

    barrier = pltpu.get_barrier_semaphore()

    def greet_z(place, carry):
        there = mod(z + distance(place), nz)
        for core in range(nc):
            pl.semaphore_signal(barrier, 1, device_id={"z": there, "c": core}, device_id_type=MESH)
        return carry

    lax.fori_loop(1, nz, greet_z, 0)
    pl.semaphore_signal(barrier, 1, device_id={"c": 1 - c}, device_id_type=MESH)
    for step in range(1, nx):
        pl.semaphore_signal(barrier, 1, device_id={"x": mod(x + step, nx)}, device_id_type=MESH)
    for step in range(1, nr):
        pl.semaphore_signal(barrier, 1, device_id={"rep": mod(r + step, nr)}, device_id_type=MESH)

    def momentum_block(m, carry):
        value = MOMENTUM_DECAY * momentum_ref[m] + grads_ref[m].astype(jnp.float32)
        new_momentum_ref[m] = value
        half[m] = value.astype(jnp.bfloat16)
        return carry

    def code_block(m, carry):
        value = master_ref[m]
        level = jnp.sqrt(jnp.sqrt(jnp.abs(value) * (1.0 / MASTER_BOUND)))
        code = (jnp.minimum(level, 1.0) * CODE_TOP + 0.5).astype(jnp.int32)
        codes[m] = jnp.where(value < 0, -code, code).astype(jnp.int16)
        return carry

    loads[0].wait()
    loads[1].wait()
    lax.fori_loop(0, count, momentum_block, 0, unroll=4)
    pl.semaphore_wait(barrier, (nz - 1) * nc + 1 + (nx - 1) + (nr - 1))

    def to_slabs(source, target, phase, core):
        def send(place, carry):
            there = mod(z + distance(place), nz)
            pltpu.make_async_remote_copy(
                source.at[nc * there + core],
                target.at[x, place * nc + c],
                send_sem.at[phase],
                slab_sem.at[phase, place // per_chunk],
                device_id={"z": there, "c": core},
                device_id_type=MESH,
            ).start()
            return carry

        @pl.when(c == core)
        def _():
            pltpu.make_async_copy(
                source.at[nc * z + core], target.at[x, c], slab_sem.at[phase, 0]
            ).start()

        @pl.when(c != core)
        def _():
            send(0, 0)

        lax.fori_loop(1, nz, send, 0)

    def forward_x(target, phase, chunk):
        width = slots // CHUNKS
        part = target.at[x, pl.ds(chunk * width, width)]
        wait(part, slab_sem.at[phase, chunk])
        for step in (1, nx - 1, 2):
            pltpu.make_async_remote_copy(
                part,
                part,
                send_sem.at[2 + phase],
                gather_sem.at[phase],
                device_id={"x": mod(x + step, nx)},
                device_id_type=MESH,
            ).start()

    def gathered(target, phase):
        wait(target.at[pl.ds(0, nx - 1)], gather_sem.at[phase])

    def from_slab(source, target, row, phase, sems, low, high):
        def send_to(place, core):
            there = mod(z - distance(place) + nz, nz)
            pltpu.make_async_remote_copy(
                source.at[place * nc + core],
                target.at[*row],
                send_sem.at[phase],
                sems(place),
                device_id={"z": there, "c": core},
                device_id_type=MESH,
            ).start()

        if low == 0:
            pltpu.make_async_copy(source.at[c], target.at[*row], sems(0)).start()
            send_to(0, 1 - c)

        def send(place, carry):
            for core in range(nc):
                send_to(place, core)
            return carry

        lax.fori_loop(max(1, low), high, send, 0)

    for core in range(nc):
        to_slabs(half, rows_in, 0, core)
    loads[2].wait()
    lax.fori_loop(0, count, code_block, 0, unroll=4)
    for core in range(nc):
        to_slabs(codes, codes_in, 1, core)
    momentum_store = pltpu.make_async_copy(new_momentum_ref, new_momentum_hbm, store_sem.at[0])
    momentum_store.start()
    for chunk in range(CHUNKS):
        forward_x(rows_in, 0, chunk)
    gathered(rows_in, 0)

    part = slots * row_count
    total = jnp.zeros((row_count, feats), jnp.float32)
    for g in range(nx):

        def squares(b, acc):
            blocks = rows_in[g, pl.ds(b * 4, 4)].astype(jnp.float32)
            return acc + jnp.sum(blocks * blocks, axis=0)

        total = lax.fori_loop(0, slots // 4, squares, total)
    norm = jnp.sqrt(jnp.sum(total, keepdims=True))
    norm_out[...] = jnp.broadcast_to(norm, norm_out.shape)
    inverse = 1.0 / (norm + EPSILON)
    matrix_here = nc * z + c

    def send_norm(place, core):
        pltpu.make_async_remote_copy(
            norm_out,
            norms_ref.at[matrix_here],
            send_sem.at[7],
            norm_sem,
            device_id={"z": mod(z + distance(place), nz), "c": core},
            device_id_type=MESH,
        ).start()

    for g in range(nx):

        def scaled(b, carry):
            blocks = rows_in[g, pl.ds(b * 4, 4)].astype(jnp.float32) * inverse
            first = pl.multiple_of(g * part + b * 4 * row_count, 4 * row_count)
            iterate[pl.ds(first, 4 * row_count), :] = blocks.reshape(4 * row_count, feats).astype(jnp.bfloat16)
            return carry

        lax.fori_loop(0, slots // 4, scaled, 0)

    def gram_matrix():
        for j in range(feats // TILE):
            tile = pl.ds(j * TILE, TILE)
            gram[tile, :] = lax.dot_general(
                iterate[:, tile], iterate[...], (((0,), (0,)), ((), ())), preferred_element_type=jnp.float32
            ).astype(jnp.bfloat16)

    def polynomial():
        for i in range(feats // TILE):
            tile = pl.ds(i * TILE, TILE)
            rows = gram[tile, :]
            poly[tile, :] = (
                COEF_SECOND * rows.astype(jnp.float32)
                + COEF_THIRD * jnp.dot(rows, gram[...], preferred_element_type=jnp.float32)
            ).astype(jnp.bfloat16)

    def product(rows):
        return (
            COEF_FIRST * rows.astype(jnp.float32) + jnp.dot(rows, poly[...], preferred_element_type=jnp.float32)
        ).astype(jnp.bfloat16)

    def as_blocks(rows):
        return rows.astype(jnp.float32).reshape(-1, row_count, feats).astype(jnp.bfloat16)

    def all_rows(b, carry):
        tile = pl.ds(pl.multiple_of(b * TILE, TILE), TILE)
        iterate[tile, :] = product(iterate[tile, :])
        return carry

    for step in range(ITERS - 1):
        gram_matrix()
        polynomial()
        lax.fori_loop(0, groups * row_count // TILE, all_rows, 0)
    gram_matrix()
    polynomial()
    own = pl.ds(pl.multiple_of(x * part, part), part)
    update_out[...] = as_blocks(product(iterate[own, :]))

    for chunk in range(CHUNKS):
        wait(codes_in.at[x, pl.ds(chunk * (slots // CHUNKS), slots // CHUNKS)], slab_sem.at[1, chunk])
    scale = 0.2 * math.sqrt(max(groups * row_count, feats))

    def updated(old, update):
        return old - LEARN_RATE * (scale * update.astype(jnp.float32) + DECAY_RATE * old)

    offset = offsets_ref[r * count + matrix_here]

    def weight_block(slot, carry):
        place, core = slot // nc, lax.rem(slot, nc)
        true_low = mod(z - distance(place) + nz, nz) * nc + core
        stored = lax.rem(true_low - lax.rem(offset, slots) + slots, slots)
        source = place_of(mod(z - stored // nc + nz, nz)) * nc + lax.rem(stored, nc)
        code = codes_in[x, source].astype(jnp.float32)
        level = jnp.square(code * (1.0 / CODE_TOP))
        old = jnp.where(code < 0, -MASTER_BOUND, MASTER_BOUND) * jnp.square(level)
        picked[slot] = updated(old, update_out[source]).astype(jnp.bfloat16)
        return carry

    lax.fori_loop(0, slots, weight_block, 0, unroll=2)
    from_slab(picked, shifted, (x, matrix_here), 5, lambda place: true_sem.at[c, place // per_chunk], 0, nz)
    from_slab(update_out, update_in, (matrix_here,), 4, lambda place: back_sem.at[c], 0, nz)
    pltpu.make_async_copy(norm_out, norms_ref.at[matrix_here], norm_sem).start()
    send_norm(0, 1 - c)

    def norm_loop(place, carry):
        for core in range(nc):
            send_norm(place, core)
        return carry

    lax.fori_loop(1, nz, norm_loop, 0)


    def each(chunk, act):
        def one(place, carry):
            for core in range(nc):
                act(nc * mod(z + distance(place), nz) + core)
            return carry

        lax.fori_loop(chunk * per_chunk, (chunk + 1) * per_chunk, one, 0)

    def spread_x(m, sem):
        for step in (2, 1, nx - 1):
            pltpu.make_async_remote_copy(
                shifted.at[x, m],
                shifted.at[x, m],
                send_sem.at[3],
                sem,
                device_id={"x": mod(x + step, nx)},
                device_id_type=MESH,
            ).start()

    def spread_rep(m):
        row = r * count + m
        for step in (2, 1, nr - 1):
            pltpu.make_async_remote_copy(
                weights_ref.at[row],
                weights_ref.at[row],
                send_sem.at[6],
                rep_sem,
                device_id={"rep": mod(r + step, nr)},
                device_id_type=MESH,
            ).start()

    own_index = (x * nz + z) * nc + c

    def pick(m):
        stored = lax.rem(own_index - offsets_ref[r * count + m] + groups, groups)
        value = shifted[0, m]
        for group in range(1, nx):
            value = jnp.where(stored // slots == group, shifted[group, m], value)
        weights_ref[r * count + m] = value

    for turn in range(CHUNKS + 2):
        if turn < CHUNKS:
            for core in range(nc):
                wait(picked.at[pl.ds(0, per_chunk)], true_sem.at[core, turn])
            each(turn, lambda m: spread_x(m, shift_sem.at[turn]))
        if 1 <= turn <= CHUNKS:
            wait(picked.at[pl.ds(0, (nx - 1) * nc * per_chunk)], shift_sem.at[turn - 1])
            each(turn - 1, pick)
        if turn >= 2:
            each(turn - 2, spread_rep)

    for core in range(nc):
        wait(update_in.at[pl.ds(0, nz)], back_sem.at[core])

    def master_block(m, carry):
        new_master_ref[m] = updated(master_ref[m], update_in[m])
        return carry

    lax.fori_loop(0, count, master_block, 0, unroll=4)
    master_store = pltpu.make_async_copy(new_master_ref, new_master_hbm, store_sem.at[2])
    master_store.start()
    wait(weights_ref.at[pl.ds(0, (nr - 1) * count)], rep_sem)
    weights_store = pltpu.make_async_copy(weights_ref, weights_hbm, store_sem.at[1])
    weights_store.start()

    wait(norms_ref, norm_sem)
    def slot_value(m, total):
        return total + jnp.where(owners_ref[r * count + m] == own_index, norms_ref[m], 0.0)

    slot = lax.fori_loop(0, count, slot_value, jnp.zeros(norm_out.shape, jnp.float32), unroll=8)
    slot_ref[...] = slot[:, :1] / math.sqrt(groups * row_count * feats)
    for phase, array in ((0, half), (1, codes), (4, update_out), (5, picked)):
        wait(array.at[pl.ds(0, count - 1)], send_sem.at[phase])
    wait(rows_in.at[pl.ds(0, nx - 1)], send_sem.at[2])
    wait(shifted.at[pl.ds(0, nx - 1)], send_sem.at[3])
    wait(weights_ref.at[pl.ds(0, (nr - 1) * count)], send_sem.at[6])
    wait(norms_ref.at[pl.ds(0, count - 1)], send_sem.at[7])
    momentum_store.wait()
    weights_store.wait()
    master_store.wait()


def on_device(grads, momentum, master, owners, offsets):
    nx, nz, nc, nr = (lax.axis_size(a) for a in ("x", "z", "c", "rep"))
    groups = nx * nz * nc
    count, rows, feats = grads.shape
    blocks = (count, rows, feats)
    whole = (nx, count, rows, feats)
    everything = (nr * count, rows, feats)
    vmem = pl.BlockSpec(memory_space=pltpu.VMEM)
    smem = pl.BlockSpec(memory_space=pltpu.SMEM)
    away = pl.BlockSpec(memory_space=pl.ANY)
    return pl.pallas_call(
        lambda *refs: kernel((nx, nz, nc, nr), *refs),
        out_shape=(
            jax.ShapeDtypeStruct(blocks, jnp.float32),
            jax.ShapeDtypeStruct(blocks, jnp.float32),
            jax.ShapeDtypeStruct(everything, jnp.bfloat16),
            jax.ShapeDtypeStruct((1, 1), jnp.float32),
        ),
        in_specs=[smem, smem, away, away, away],
        out_specs=(away, away, away, vmem),
        scratch_shapes=[
            pltpu.VMEM(blocks, jnp.bfloat16),
            pltpu.VMEM(blocks, jnp.float32),
            pltpu.VMEM(blocks, jnp.float32),
            pltpu.VMEM(blocks, jnp.float32),
            pltpu.VMEM(blocks, jnp.float32),
            pltpu.VMEM(everything, jnp.bfloat16),
            pltpu.VMEM((count, 1, 128), jnp.float32),
            pltpu.VMEM(blocks, jnp.bfloat16),
            pltpu.VMEM(whole, jnp.bfloat16),
            pltpu.VMEM((groups * rows, feats), jnp.bfloat16),
            pltpu.VMEM((feats, feats), jnp.bfloat16),
            pltpu.VMEM((feats, feats), jnp.bfloat16),
            pltpu.VMEM(whole, jnp.bfloat16),
            pltpu.VMEM(blocks, jnp.bfloat16),
            pltpu.VMEM(blocks, jnp.bfloat16),
            pltpu.VMEM(blocks, jnp.int16),
            pltpu.VMEM(whole, jnp.int16),
            pltpu.VMEM(blocks, jnp.bfloat16),
            pltpu.VMEM((1, 128), jnp.float32),
            pltpu.SemaphoreType.DMA((8,)),
            pltpu.SemaphoreType.DMA((2, CHUNKS)),
            pltpu.SemaphoreType.DMA((2,)),
            pltpu.SemaphoreType.DMA((nc,)),
            pltpu.SemaphoreType.DMA((nc, CHUNKS)),
            pltpu.SemaphoreType.DMA,
            pltpu.SemaphoreType.DMA((CHUNKS,)),
            pltpu.SemaphoreType.DMA,
            pltpu.SemaphoreType.DMA((3,)),
            pltpu.SemaphoreType.DMA((3,)),
        ],
        compiler_params=pltpu.CompilerParams(
            collective_id=0, has_side_effects=True, vmem_limit_bytes=60 * 1024 * 1024
        ),
        name="muon_step",
    )(offsets, owners, grads, momentum, master)


def solution(mesh):
    fine = Mesh(mesh.devices.reshape(4, 16, 2, 4), ("x", "z", "c", "rep"))
    rows = ("x", "z", "c")
    split = P("rep", rows, None)
    in_specs = (split, split, split, P(), P())
    out_specs = (split, split, P(None, rows, None), P(rows, "rep"))
    return jax.shard_map(on_device, mesh=fine, in_specs=in_specs, out_specs=out_specs, check_vma=False)
```

```python
import math

import jax
import jax.numpy as jnp
from jax import lax
from jax.experimental import pallas as pl
from jax.experimental.pallas import tpu as pltpu
from jax.sharding import Mesh, PartitionSpec as P

ITERS = 2

COEF_FIRST = 3.4445
COEF_SECOND = -4.775
COEF_THIRD = 2.0315
MOMENTUM_DECAY = 0.95
LEARN_RATE = 0.02
DECAY_RATE = 0.1
EPSILON = 1e-07
MESH = pl.DeviceIdType.MESH
TILE = 256
CHUNKS = 16
MASTER_BOUND = 0.1875
CODE_TOP = 32767.0


def kernel(
    sizes,
    offsets_ref,
    owners_ref,
    grads_hbm,
    momentum_hbm,
    master_hbm,
    new_momentum_hbm,
    new_master_hbm,
    weights_hbm,
    slot_ref,
    grads_ref,
    momentum_ref,
    master_ref,
    new_momentum_ref,
    new_master_ref,
    weights_ref,
    norms_ref,
    half,
    rows_in,
    iterate,
    gram,
    poly,
    shifted,
    update_out,
    update_in,
    codes,
    codes_in,
    picked,
    norm_out,
    send_sem,
    slab_sem,
    gather_sem,
    back_sem,
    true_sem,
    rep_sem,
    shift_sem,
    norm_sem,
    load_sem,
    store_sem,
):
    nx, nz, nc, nr = sizes
    x, z, c, r = (lax.axis_index(a) for a in ("x", "z", "c", "rep"))
    groups = nx * nz * nc
    count, row_count, feats = half.shape
    slots = nz * nc
    per_chunk = nz // CHUNKS

    def distance(place):
        near = nz - place
        far = jnp.where(near % 2 == 1, nz - (near + 1) // 2, near // 2)
        return jnp.where(place == 0, 0, far)

    def place_of(hops):
        near = jnp.where(hops < nz // 2, 2 * hops, jnp.where(hops == nz // 2, nz - 1, 2 * (nz - hops) - 1))
        return jnp.where(hops == 0, 0, nz - near)

    def mod(a, n):
        return lax.rem(a + n, n)

    def wait(ref, sem):
        pltpu.make_async_copy(ref, ref, sem).wait()

    loads = [
        pltpu.make_async_copy(source, target, load_sem.at[i])
        for i, (source, target) in enumerate(
            ((grads_hbm, grads_ref), (momentum_hbm, momentum_ref), (master_hbm, master_ref))
        )
    ]
    for load in loads:
        load.start()

    barrier = pltpu.get_barrier_semaphore()

    def greet_z(place, carry):
        there = mod(z + distance(place), nz)
        for core in range(nc):
            pl.semaphore_signal(barrier, 1, device_id={"z": there, "c": core}, device_id_type=MESH)
        return carry

    lax.fori_loop(1, nz, greet_z, 0)
    pl.semaphore_signal(barrier, 1, device_id={"c": 1 - c}, device_id_type=MESH)
    for step in range(1, nx):
        pl.semaphore_signal(barrier, 1, device_id={"x": mod(x + step, nx)}, device_id_type=MESH)
    for step in range(1, nr):
        pl.semaphore_signal(barrier, 1, device_id={"rep": mod(r + step, nr)}, device_id_type=MESH)

    def momentum_block(m, carry):
        value = MOMENTUM_DECAY * momentum_ref[m] + grads_ref[m].astype(jnp.float32)
        new_momentum_ref[m] = value
        half[m] = value.astype(jnp.bfloat16)
        return carry

    def code_block(m, carry):
        value = master_ref[m]
        level = jnp.sqrt(jnp.sqrt(jnp.abs(value) * (1.0 / MASTER_BOUND)))
        code = (jnp.minimum(level, 1.0) * CODE_TOP + 0.5).astype(jnp.int32)
        codes[m] = jnp.where(value < 0, -code, code).astype(jnp.int16)
        return carry

    loads[0].wait()
    loads[1].wait()
    lax.fori_loop(0, count, momentum_block, 0, unroll=4)
    pl.semaphore_wait(barrier, (nz - 1) * nc + 1 + (nx - 1) + (nr - 1))

    def to_slabs(source, target, phase, core):
        def send(place, carry):
            there = mod(z + distance(place), nz)
            pltpu.make_async_remote_copy(
                source.at[nc * there + core],
                target.at[x, place * nc + c],
                send_sem.at[phase],
                slab_sem.at[phase, place // per_chunk],
                device_id={"z": there, "c": core},
                device_id_type=MESH,
            ).start()
            return carry

        @pl.when(c == core)
        def _():
            pltpu.make_async_copy(
                source.at[nc * z + core], target.at[x, c], slab_sem.at[phase, 0]
            ).start()

        @pl.when(c != core)
        def _():
            send(0, 0)

        lax.fori_loop(1, nz, send, 0)

    def forward_x(target, phase, chunk):
        width = slots // CHUNKS
        part = target.at[x, pl.ds(chunk * width, width)]
        wait(part, slab_sem.at[phase, chunk])
        for step in (1, nx - 1, 2):
            pltpu.make_async_remote_copy(
                part,
                part,
                send_sem.at[2 + phase],
                gather_sem.at[phase],
                device_id={"x": mod(x + step, nx)},
                device_id_type=MESH,
            ).start()

    def gathered(target, phase):
        wait(target.at[pl.ds(0, nx - 1)], gather_sem.at[phase])

    def from_slab(source, target, row, phase, sems, low, high):
        def send_to(place, core):
            there = mod(z - distance(place) + nz, nz)
            pltpu.make_async_remote_copy(
                source.at[place * nc + core],
                target.at[*row],
                send_sem.at[phase],
                sems(place),
                device_id={"z": there, "c": core},
                device_id_type=MESH,
            ).start()

        if low == 0:
            pltpu.make_async_copy(source.at[c], target.at[*row], sems(0)).start()
            send_to(0, 1 - c)

        def send(place, carry):
            for core in range(nc):
                send_to(place, core)
            return carry

        lax.fori_loop(max(1, low), high, send, 0)

    for core in range(nc):
        to_slabs(half, rows_in, 0, core)
    loads[2].wait()
    lax.fori_loop(0, count, code_block, 0, unroll=4)
    for core in range(nc):
        to_slabs(codes, codes_in, 1, core)
    momentum_store = pltpu.make_async_copy(new_momentum_ref, new_momentum_hbm, store_sem.at[0])
    momentum_store.start()
    for chunk in range(CHUNKS):
        forward_x(rows_in, 0, chunk)
    gathered(rows_in, 0)

    part = slots * row_count
    total = jnp.zeros((row_count, feats), jnp.float32)
    for g in range(nx):

        def squares(b, acc):
            blocks = rows_in[g, pl.ds(b * 4, 4)].astype(jnp.float32)
            return acc + jnp.sum(blocks * blocks, axis=0)

        total = lax.fori_loop(0, slots // 4, squares, total)
    norm = jnp.sqrt(jnp.sum(total, keepdims=True))
    norm_out[...] = jnp.broadcast_to(norm, norm_out.shape)
    inverse = 1.0 / (norm + EPSILON)
    matrix_here = nc * z + c

    def send_norm(place, core):
        pltpu.make_async_remote_copy(
            norm_out,
            norms_ref.at[matrix_here],
            send_sem.at[7],
            norm_sem,
            device_id={"z": mod(z + distance(place), nz), "c": core},
            device_id_type=MESH,
        ).start()

    for g in range(nx):

        def scaled(b, carry):
            blocks = rows_in[g, pl.ds(b * 4, 4)].astype(jnp.float32) * inverse
            first = pl.multiple_of(g * part + b * 4 * row_count, 4 * row_count)
            iterate[pl.ds(first, 4 * row_count), :] = blocks.reshape(4 * row_count, feats).astype(jnp.bfloat16)
            return carry

        lax.fori_loop(0, slots // 4, scaled, 0)

    def gram_matrix():
        for j in range(feats // TILE):
            tile = pl.ds(j * TILE, TILE)
            gram[tile, :] = lax.dot_general(
                iterate[:, tile], iterate[...], (((0,), (0,)), ((), ())), preferred_element_type=jnp.float32
            ).astype(jnp.bfloat16)

    def polynomial():
        for i in range(feats // TILE):
            tile = pl.ds(i * TILE, TILE)
            rows = gram[tile, :]
            poly[tile, :] = (
                COEF_SECOND * rows.astype(jnp.float32)
                + COEF_THIRD * jnp.dot(rows, gram[...], preferred_element_type=jnp.float32)
            ).astype(jnp.bfloat16)

    def product(rows):
        return (
            COEF_FIRST * rows.astype(jnp.float32) + jnp.dot(rows, poly[...], preferred_element_type=jnp.float32)
        ).astype(jnp.bfloat16)

    def as_blocks(rows):
        return rows.astype(jnp.float32).reshape(-1, row_count, feats).astype(jnp.bfloat16)

    def all_rows(b, carry):
        tile = pl.ds(pl.multiple_of(b * TILE, TILE), TILE)
        iterate[tile, :] = product(iterate[tile, :])
        return carry

    for step in range(ITERS - 1):
        gram_matrix()
        polynomial()
        lax.fori_loop(0, groups * row_count // TILE, all_rows, 0)
    gram_matrix()
    polynomial()
    own = pl.ds(pl.multiple_of(x * part, part), part)
    update_out[...] = as_blocks(product(iterate[own, :]))

    for chunk in range(CHUNKS):
        wait(codes_in.at[x, pl.ds(chunk * (slots // CHUNKS), slots // CHUNKS)], slab_sem.at[1, chunk])
    scale = 0.2 * math.sqrt(max(groups * row_count, feats))

    def updated(old, update):
        return old - LEARN_RATE * (scale * update.astype(jnp.float32) + DECAY_RATE * old)

    offset = offsets_ref[r * count + matrix_here]

    def weight_block(slot, carry):
        place, core = slot // nc, lax.rem(slot, nc)
        true_low = mod(z - distance(place) + nz, nz) * nc + core
        stored = lax.rem(true_low - lax.rem(offset, slots) + slots, slots)
        source = place_of(mod(z - stored // nc + nz, nz)) * nc + lax.rem(stored, nc)
        code = codes_in[x, source].astype(jnp.float32)
        level = jnp.square(code * (1.0 / CODE_TOP))
        old = jnp.where(code < 0, -MASTER_BOUND, MASTER_BOUND) * jnp.square(level)
        picked[slot] = updated(old, update_out[source]).astype(jnp.bfloat16)
        return carry

    lax.fori_loop(0, slots, weight_block, 0, unroll=2)
    from_slab(picked, shifted, (x, matrix_here), 5, lambda place: true_sem.at[c, place // per_chunk], 0, nz)
    from_slab(update_out, update_in, (matrix_here,), 4, lambda place: back_sem.at[c], 0, nz)
    pltpu.make_async_copy(norm_out, norms_ref.at[matrix_here], norm_sem).start()
    send_norm(0, 1 - c)

    def norm_loop(place, carry):
        for core in range(nc):
            send_norm(place, core)
        return carry

    lax.fori_loop(1, nz, norm_loop, 0)


    def each(chunk, act):
        def one(place, carry):
            for core in range(nc):
                act(nc * mod(z + distance(place), nz) + core)
            return carry

        lax.fori_loop(chunk * per_chunk, (chunk + 1) * per_chunk, one, 0)

    def spread_x(m, sem):
        for step in (2, 1, nx - 1):
            pltpu.make_async_remote_copy(
                shifted.at[x, m],
                shifted.at[x, m],
                send_sem.at[3],
                sem,
                device_id={"x": mod(x + step, nx)},
                device_id_type=MESH,
            ).start()

    def spread_rep(m):
        row = r * count + m
        for step in (2, 1, nr - 1):
            pltpu.make_async_remote_copy(
                weights_ref.at[row],
                weights_ref.at[row],
                send_sem.at[6],
                rep_sem,
                device_id={"rep": mod(r + step, nr)},
                device_id_type=MESH,
            ).start()

    own_index = (x * nz + z) * nc + c

    def pick(m):
        stored = lax.rem(own_index - offsets_ref[r * count + m] + groups, groups)
        value = shifted[0, m]
        for group in range(1, nx):
            value = jnp.where(stored // slots == group, shifted[group, m], value)
        weights_ref[r * count + m] = value

    for turn in range(CHUNKS + 2):
        if turn < CHUNKS:
            for core in range(nc):
                wait(picked.at[pl.ds(0, per_chunk)], true_sem.at[core, turn])
            each(turn, lambda m: spread_x(m, shift_sem.at[turn]))
        if 1 <= turn <= CHUNKS:
            wait(picked.at[pl.ds(0, (nx - 1) * nc * per_chunk)], shift_sem.at[turn - 1])
            each(turn - 1, pick)
        if turn >= 2:
            each(turn - 2, spread_rep)

    for core in range(nc):
        wait(update_in.at[pl.ds(0, nz)], back_sem.at[core])

    def master_block(m, carry):
        new_master_ref[m] = updated(master_ref[m], update_in[m])
        return carry

    lax.fori_loop(0, count, master_block, 0, unroll=4)
    master_store = pltpu.make_async_copy(new_master_ref, new_master_hbm, store_sem.at[2])
    master_store.start()
    wait(weights_ref.at[pl.ds(0, (nr - 1) * count)], rep_sem)
    weights_store = pltpu.make_async_copy(weights_ref, weights_hbm, store_sem.at[1])
    weights_store.start()

    wait(norms_ref, norm_sem)
    def slot_value(m, total):
        return total + jnp.where(owners_ref[r * count + m] == own_index, norms_ref[m], 0.0)

    slot = lax.fori_loop(0, count, slot_value, jnp.zeros(norm_out.shape, jnp.float32), unroll=8)
    slot_ref[...] = slot[:, :1] / math.sqrt(groups * row_count * feats)
    for phase, array in ((0, half), (1, codes), (4, update_out), (5, picked)):
        wait(array.at[pl.ds(0, count - 1)], send_sem.at[phase])
    wait(rows_in.at[pl.ds(0, nx - 1)], send_sem.at[2])
    wait(shifted.at[pl.ds(0, nx - 1)], send_sem.at[3])
    wait(weights_ref.at[pl.ds(0, (nr - 1) * count)], send_sem.at[6])
    wait(norms_ref.at[pl.ds(0, count - 1)], send_sem.at[7])
    momentum_store.wait()
    weights_store.wait()
    master_store.wait()


def on_device(grads, momentum, master, owners, offsets):
    nx, nz, nc, nr = (lax.axis_size(a) for a in ("x", "z", "c", "rep"))
    groups = nx * nz * nc
    count, rows, feats = grads.shape
    blocks = (count, rows, feats)
    whole = (nx, count, rows, feats)
    everything = (nr * count, rows, feats)
    vmem = pl.BlockSpec(memory_space=pltpu.VMEM)
    smem = pl.BlockSpec(memory_space=pltpu.SMEM)
    away = pl.BlockSpec(memory_space=pl.ANY)
    return pl.pallas_call(
        lambda *refs: kernel((nx, nz, nc, nr), *refs),
        out_shape=(
            jax.ShapeDtypeStruct(blocks, jnp.float32),
            jax.ShapeDtypeStruct(blocks, jnp.float32),
            jax.ShapeDtypeStruct(everything, jnp.bfloat16),
            jax.ShapeDtypeStruct((1, 1), jnp.float32),
        ),
        in_specs=[smem, smem, away, away, away],
        out_specs=(away, away, away, vmem),
        scratch_shapes=[
            pltpu.VMEM(blocks, jnp.bfloat16),
            pltpu.VMEM(blocks, jnp.float32),
            pltpu.VMEM(blocks, jnp.float32),
            pltpu.VMEM(blocks, jnp.float32),
            pltpu.VMEM(blocks, jnp.float32),
            pltpu.VMEM(everything, jnp.bfloat16),
            pltpu.VMEM((count, 1, 128), jnp.float32),
            pltpu.VMEM(blocks, jnp.bfloat16),
            pltpu.VMEM(whole, jnp.bfloat16),
            pltpu.VMEM((groups * rows, feats), jnp.bfloat16),
            pltpu.VMEM((feats, feats), jnp.bfloat16),
            pltpu.VMEM((feats, feats), jnp.bfloat16),
            pltpu.VMEM(whole, jnp.bfloat16),
            pltpu.VMEM(blocks, jnp.bfloat16),
            pltpu.VMEM(blocks, jnp.bfloat16),
            pltpu.VMEM(blocks, jnp.int16),
            pltpu.VMEM(whole, jnp.int16),
            pltpu.VMEM(blocks, jnp.bfloat16),
            pltpu.VMEM((1, 128), jnp.float32),
            pltpu.SemaphoreType.DMA((8,)),
            pltpu.SemaphoreType.DMA((2, CHUNKS)),
            pltpu.SemaphoreType.DMA((2,)),
            pltpu.SemaphoreType.DMA((nc,)),
            pltpu.SemaphoreType.DMA((nc, CHUNKS)),
            pltpu.SemaphoreType.DMA,
            pltpu.SemaphoreType.DMA((CHUNKS,)),
            pltpu.SemaphoreType.DMA,
            pltpu.SemaphoreType.DMA((3,)),
            pltpu.SemaphoreType.DMA((3,)),
        ],
        compiler_params=pltpu.CompilerParams(
            collective_id=0, has_side_effects=True, vmem_limit_bytes=60 * 1024 * 1024
        ),
        name="muon_step",
    )(offsets, owners, grads, momentum, master)


def solution(mesh):
    fine = Mesh(mesh.devices.reshape(4, 16, 2, 4), ("x", "z", "c", "rep"))
    rows = ("x", "z", "c")
    split = P("rep", rows, None)
    in_specs = (split, split, split, P(), P())
    out_specs = (split, split, P(None, rows, None), P(rows, "rep"))
    return jax.shard_map(on_device, mesh=fine, in_specs=in_specs, out_specs=out_specs, check_vma=False)
```
